32 devices in a mesh: group: 2 (over y), row: 4 (over z), src: 4 (over x, core).
Axes of the slice: x: 2, y: 2, z: 4, core: 2. Of those that a mesh axis runs over, the one named last changes fastest.
Arguments:
- right_side: bfloat16 [5120, 1536], P(('group', 'row'), 'src'), parts along dimension 0, may hold values from -6 to 6
- factor: bfloat16 [5120, 2048], P(('group', 'row')), parts along dimension 0, may hold values from -0.1875 to 0.1875
- pattern: int32 [40, 16], P(('group', 'row')), parts along dimension 0, may hold values 0 or 1
- inverses: bfloat16 [8, 512, 512], P('group', 'src'), parts along dimension 0, may hold values from -4 to 4
- owners: int32 [8], P('group'), parts along dimension 0, may hold values from 0 to 3, as said below
- offsets: int32 [8], P('group'), parts along dimension 0, may hold values from 0 to 1
Outputs:
- solved: bfloat16 [4096, 1536], P(('group', 'row'), 'src'), parts along dimension 0
- updated: bfloat16 [5120, 1536], P(('group', 'row'), 'src'), parts along dimension 0
The draws below stay inside these ranges and needn't reach their ends.
There are 2 independent parts, one for each index of `group`. The reference program is written for one: setup_inputs(seed, part) draws one part's arguments, and reference() takes and returns one part's arrays. A program takes and returns all parts, laid end to end along the dimension named above; each array names one. Nothing has to cross between parts.
Inputs may be any that keep to these rules, and one draw needn't show every extreme that they name: The 4 owners are different row indices, and the first and the last row index are always among them.
All inputs are finite; a program needn't handle non-finite values. No bound on the sum of `pattern` on one device may be relied on, other than what follows from the above.
Results may differ from the reference program's by a relative error of at most 0.0057.
Values may be sent and summed in bfloat16 or wider, within the bound.
A program may use at most 64 MiB of HBM per device.

```python
import jax
import jax.numpy as jnp
from jax import lax

SN = 4
SNR = 512
BLK = 128
R_DEV = 640
ROWS = 2560
SOURCES = 1536
COLS = 2048
N_ROW = 4


def draw_owners(key, part):
    score_key = jax.random.fold_in(key, 1931)
    order_key = jax.random.fold_in(key, 2711)
    scores = jax.random.randint(score_key, (N_ROW - 2,), 0, 1048576, jnp.int32)
    distinct = scores * N_ROW + jnp.arange(N_ROW - 2, dtype=jnp.int32)
    order = jnp.argsort(distinct, stable=True).astype(jnp.int32)
    middle = order[:SN - 2] + 1
    chosen = jnp.concatenate([jnp.array([0, N_ROW - 1], jnp.int32), middle.astype(jnp.int32)], 0)
    placing = jax.random.permutation(order_key, SN)
    return chosen[placing].astype(jnp.int32)


def draw_inverses(key, part):
    first_key, second_key = jax.random.split(jax.random.fold_in(key, 7), 2)
    diagonal = jax.random.uniform(first_key, (SN, SNR), jnp.float32, 0.6, 1.4)
    noise = jnp.clip(jax.random.normal(second_key, (SN, SNR, SNR), jnp.float32), -4.0, 4.0) * (0.5 / SNR ** 0.5)
    matrix = noise + jnp.eye(SNR, dtype=jnp.float32)[None, :, :] * diagonal[:, :, None]
    return matrix.astype(jnp.bfloat16)


def plant(drawn, rng, smallest, top_value):
    index_at = [jax.random.randint(jax.random.fold_in(rng, axis), (), 0, length) for axis, length in enumerate(drawn.shape)]
    main_axis = drawn.shape.index(max(drawn.shape))
    neighbour = index_at[:main_axis] + [(index_at[main_axis] + 1) % drawn.shape[main_axis]] + index_at[main_axis + 1:]
    return drawn.at[tuple(index_at)].set(smallest).at[tuple(neighbour)].set(top_value)


def shard_levels(rng, shape, shards, smallest, high):
    def one(position, parts):
        steps = jax.random.uniform(jax.random.fold_in(jax.random.fold_in(rng, 6), position), (parts,), jnp.float32, smallest / len(shards), high / len(shards))
        return jnp.repeat(jnp.exp(steps), shape[position] // parts).reshape((-1,) + (1,) * (len(shape) - position - 1))

    gain = one(*shards[0])
    for cut in shards[1:]:
        gain = gain * one(*cut)
    return gain


def centred(stream_key, dims, scale, reach, shards=(), held_as=jnp.bfloat16):
    level = shard_levels(stream_key, dims, shards, -0.22, 0.18) if shards else 1.0
    values = jax.random.normal(stream_key, dims, jnp.float32) * scale * level
    return jnp.minimum(jnp.maximum(values, -reach), reach).astype(held_as)


def setup_inputs(seed: int = 0, part: int = 0) -> dict:
    keys = jax.random.split(jax.random.key(seed), 7)
    own_keys = jax.random.split(jax.random.fold_in(keys[6], part), 7)
    return {
        "right_side": centred(own_keys[0], (ROWS, SOURCES), 1.0, 6.0, ((0, 4), (1, 4))),
        "factor": centred(own_keys[1], (ROWS, COLS), (COLS // 2) ** -0.5, 0.1875, ((0, 4),)),
        "pattern": plant((jax.random.randint(own_keys[2], (ROWS // BLK, COLS // BLK), 0, 2) < 1).astype(jnp.int32), jax.random.fold_in(own_keys[2], 1), 0, 1),
        "inverses": draw_inverses(jax.random.fold_in(jax.random.fold_in(keys[6], part), 71), part),
        "owners": draw_owners(jax.random.fold_in(jax.random.fold_in(keys[6], part), 71), part),
        "offsets": plant(jax.random.randint(own_keys[5], (SN,), 0, R_DEV // BLK - SNR // BLK + 1), jax.random.fold_in(own_keys[5], 1), 0, (R_DEV // BLK - SNR // BLK + 1) - 1).astype(jnp.int32),
    }


def expanded_keep(pattern, ranking, column_node):
    row_blocks, col_blocks = pattern.shape
    tile_mask = jnp.broadcast_to((pattern > 0)[:, None, :, None], (row_blocks, BLK, col_blocks, BLK))
    tile_mask = tile_mask.reshape(row_blocks * BLK, col_blocks * BLK)
    return tile_mask & (ranking[:, None] > column_node[None, :])


def reference(right_side, factor, pattern, inverses, owners, offsets):
    row_index = jnp.arange(ROWS, dtype=jnp.int32)
    starts = (owners * R_DEV + offsets * BLK).astype(jnp.int32)
    ranking = jnp.full((ROWS,), SN, jnp.int32)
    for supernode in range(SN):
        inside = (row_index >= starts[supernode]) & (row_index < starts[supernode] + SNR)
        ranking = jnp.where(inside, jnp.int32(supernode), ranking)
    column_node = (jnp.arange(COLS, dtype=jnp.int32) // SNR).astype(jnp.int32)
    retained = expanded_keep(pattern, ranking, column_node)
    masked = jnp.where(retained, factor, jnp.zeros((), factor.dtype))
    running = right_side.astype(jnp.float32)
    pieces = []
    for supernode in range(SN):
        segment = lax.dynamic_slice(running, (starts[supernode], jnp.int32(0)), (SNR, SOURCES)).astype(jnp.bfloat16)
        solution = jnp.dot(inverses[supernode], segment, preferred_element_type=jnp.float32).astype(jnp.bfloat16)
        pieces.append(solution)
        columns = masked[:, supernode * SNR:(supernode + 1) * SNR]
        running = running - jnp.dot(columns, solution, preferred_element_type=jnp.float32)
    return jnp.concatenate(pieces, 0), running.astype(jnp.bfloat16)
```

```python
import functools

import jax
import jax.numpy as jnp
from jax import lax
from jax.experimental import pallas as pl
from jax.experimental.pallas import tpu as pltpu
from jax.sharding import PartitionSpec as P

BLK = 128
PIECES = 4
AHEAD = 4
NEAR, FAR = 0, 1
MESH = pl.DeviceIdType.MESH


def chain_kernel(
    n_row, n_src,
    pattern_in, owners_in, offsets_in, rhs_in, factor, inverses_in, solved, updated,
    pattern, owners, offsets, rhs, inverses,
    panel, whole, running, cand, recv, out, xs,
    other, first, blocks, block,
    load_sem, panel_sem, inv_send, inv_recv, blk_send, blk_recv, send_sem, recv_sem,
):
    sn, rows, snr = panel.shape
    chunks = running.shape[0]
    part = snr // PIECES
    z = lax.axis_index("row")
    s = lax.axis_index("src")
    low = z < n_row // 2
    toward = jnp.where(low, 1, -1)
    far_dev = z + toward
    near_dev = z - toward
    at_end = (z == 0) | (z == n_row - 1)
    inner = jnp.logical_not(at_end)
    crossing = (z == n_row // 2 - 1) | (z == n_row // 2)
    far_slot = jnp.where(crossing, FAR, NEAR)

    small = [
        pltpu.make_async_copy(source, target, load_sem.at[i])
        for i, (source, target) in enumerate((
            (owners_in, owners), (offsets_in, offsets), (pattern_in, pattern),
            (inverses_in, inverses), (rhs_in, rhs),
        ))
    ]
    for load in small:
        load.start()
    loads = [
        pltpu.make_async_copy(factor.at[:, pl.ds(k * snr, snr)], panel.at[k], panel_sem.at[k])
        for k in range(sn)
    ]
    for load in loads:
        load.start()

    barrier = pltpu.get_barrier_semaphore()
    pl.semaphore_signal(barrier, inc=1, device_id={"row": far_dev}, device_id_type=MESH)

    @pl.when(inner)
    def _():
        pl.semaphore_signal(barrier, inc=1, device_id={"row": near_dev}, device_id_type=MESH)

    for d in range(1, n_src):
        pl.semaphore_signal(
            barrier, inc=1, device_id={"src": lax.rem(s + d, n_src)}, device_id_type=MESH
        )

    for load in small:
        load.wait()
    mine = jnp.int32(sn)
    shift = jnp.int32(0)
    for k in range(sn):
        held = owners[k] == z
        mine = jnp.where(held, k, mine)
        shift = jnp.where(held, offsets[k], shift)
    own_rows = inverses[0]
    for k in range(1, sn):
        own_rows = jnp.where(mine == k, inverses[k], own_rows)
    whole[s] = own_rows
    for c in range(chunks):
        running[c] = rhs[:, c * BLK : (c + 1) * BLK].astype(jnp.float32)

    pl.semaphore_wait(barrier, jnp.where(at_end, n_src, n_src + 1))

    def inverse_copy(d, which):
        return pltpu.make_async_remote_copy(
            src_ref=inverses.at[1] if which else whole.at[s],
            dst_ref=other.at[s] if which else whole.at[s],
            send_sem=inv_send.at[which, d],
            recv_sem=inv_recv.at[which, s],
            device_id={"src": lax.rem(s + d, n_src)},
            device_id_type=MESH,
        )

    def inverse_arrival(d, which):
        source = lax.rem(s + n_src - d, n_src)
        held = other if which else whole
        return pltpu.make_async_remote_copy(
            src_ref=held.at[source],
            dst_ref=held.at[source],
            send_sem=inv_send.at[which, d],
            recv_sem=inv_recv.at[which, source],
            device_id={"src": source},
            device_id_type=MESH,
        )

    n_blk = snr // BLK
    b = lax.rem(s, n_blk)

    def block_copy(d):
        return pltpu.make_async_remote_copy(
            src_ref=blocks.at[b],
            dst_ref=blocks.at[b],
            send_sem=blk_send.at[d],
            recv_sem=blk_recv.at[b],
            device_id={"src": s - b + lax.rem(b + d, n_blk)},
            device_id_type=MESH,
        )

    def block_arrival(d):
        source = lax.rem(b + n_blk - d, n_blk)
        return pltpu.make_async_remote_copy(
            src_ref=blocks.at[source],
            dst_ref=blocks.at[source],
            send_sem=blk_send.at[d],
            recv_sem=blk_recv.at[source],
            device_id={"src": s - b + source},
            device_id_type=MESH,
        )

    for d in range(1, n_src):
        inverse_copy(d, 0).start()
    for d in range(1, n_src):
        inverse_copy(d, 1).start()
    other[s] = inverses[1]

    def mask(k):
        loads[k].wait()
        for t in range(rows // BLK):
            inside = (t >= shift) & (t < shift + snr // BLK)
            rank = jnp.where(inside, mine, sn)
            for j in range(snr // BLK):
                keep = (pattern[t, k * (snr // BLK) + j] > 0) & (rank > k)
                tile = panel[k, t * BLK : (t + 1) * BLK, j * BLK : (j + 1) * BLK]
                panel[k, t * BLK : (t + 1) * BLK, j * BLK : (j + 1) * BLK] = jnp.where(
                    keep, tile, jnp.zeros_like(tile)
                )

    def message(way, k, c, p):
        span = pl.ds(p * part, part)
        return pltpu.make_async_remote_copy(
            src_ref=out.at[way, k, c, span],
            dst_ref=recv.at[far_slot if way == FAR else FAR, k, c, span],
            send_sem=send_sem.at[way, k, c, p],
            recv_sem=recv_sem.at[far_slot if way == FAR else FAR, k, c, p],
            device_id={"row": far_dev if way == FAR else near_dev},
            device_id_type=MESH,
        )

    def arrival(way, k, c, p):
        span = pl.ds(p * part, part)
        return pltpu.make_async_remote_copy(
            src_ref=out.at[way, k, c, span],
            dst_ref=recv.at[way, k, c, span],
            send_sem=send_sem.at[way, k, c, p],
            recv_sem=recv_sem.at[way, k, c, p],
            device_id={"row": far_dev if way == FAR else near_dev},
            device_id_type=MESH,
        )

    def offer(k, c, value):
        cand[k, c] = value

        @pl.when(at_end)
        def _():
            out[FAR, k, c] = value
            for p in range(PIECES):
                message(FAR, k, c, p).start()

    def segment_of(read):
        found = read(0)
        for t in range(1, (rows - snr) // BLK + 1):
            found = jnp.where(shift == t, read(t * BLK), found)
        return found

    def own_segment(c):
        return segment_of(lambda t: running[c, t : t + snr]).astype(jnp.bfloat16)

    def candidate(k, c):
        offer(k, c, jnp.dot(
            whole[...].reshape(snr, snr), own_segment(c), preferred_element_type=jnp.float32
        ).astype(jnp.bfloat16))

    def node(k):
        if isinstance(k, int):
            return (1, 0)[k] if k < 2 else 1 if k == sn else k
        return k

    def forward(k, c, p, came, way):
        arrival(came, k, c, p).wait_recv()
        span = pl.ds(p * part, part)
        out[way, k, c, span] = jnp.where(
            mine == node(k), cand[k, c, span], recv[came, k, c, span]
        )
        message(way, k, c, p).start()

    opening = [(sn, 0)] + [(k, c) for c in range(chunks) for k in (0, 1)]

    def near_forward(k, place):
        c, p = divmod(place, PIECES)
        if isinstance(k, int):
            later = opening.index((k, 0)) + c if k == sn else c
            k, c = opening[later] if later < len(opening) else (2, later - len(opening))
            forward(k, c, p, NEAR, FAR)
        elif c < chunks:
            forward(k, c, p, NEAR, FAR)
        else:
            @pl.when(k + 1 < sn)
            def _():
                forward(k + 1, c - chunks, p, NEAR, FAR)

    def exchange(k, c):
        @pl.when(inner)
        def _():
            for p in range(PIECES):
                base = opening.index((k, c)) if isinstance(k, int) else c
                near_forward(sn if isinstance(k, int) else k, base * PIECES + p + AHEAD)
                forward(k, c, p, FAR, NEAR)

        @pl.when(at_end)
        def _():
            for p in range(PIECES):
                arrival(FAR, k, c, p).wait_recv()

    def pick(k, c):
        owner = owners[node(k)]
        from_near = jnp.where(low, z - owner, owner - z) > 0
        return jnp.where(
            mine == node(k),
            cand[k, c],
            jnp.where(from_near, recv[NEAR, k, c], recv[FAR, k, c]),
        )

    def update(k, c, x):
        begin = k * snr if isinstance(k, int) else pl.multiple_of(k * snr, snr)
        xs[c, pl.ds(begin, snr)] = x
        running[c] = running[c] - jnp.dot(panel[k], x, preferred_element_type=jnp.float32)

    @pl.when(at_end)
    def _():
        recv[NEAR] = jnp.zeros_like(recv[NEAR])

    mask(0)
    stored = segment_of(lambda t: panel[0, t : t + snr, :BLK])
    for j in range(1, n_blk):
        column = segment_of(lambda t: panel[0, t : t + snr, j * BLK : (j + 1) * BLK])
        stored = jnp.where(b == j, column, stored)
    offer(sn, 0, stored)
    offer(0, 0, own_segment(0))
    for d in range(1, n_src):
        inverse_arrival(d, 0).wait_recv()
    for c in range(chunks):
        if c > 0:
            offer(0, c, own_segment(c))
        candidate(1, c)

    @pl.when(inner)
    def _():
        for place in range(AHEAD):
            near_forward(sn, place)

    exchange(sn, 0)
    blocks[b] = pick(sn, 0)
    for d in range(1, n_blk):
        block_copy(d).start()
    for k in range(1, sn):
        mask(k)
    for c in range(chunks):
        exchange(0, c)
        first[c] = pick(0, c)
        exchange(1, c)
        if c == 0:
            for d in range(1, n_src):
                inverse_arrival(d, 1).wait_recv()
            for d in range(1, n_blk):
                block_arrival(d).wait_recv()
            for j in range(n_blk):
                block[:, j * BLK : (j + 1) * BLK] = blocks[j]
        x = pick(1, c)
        segment = first[c].astype(jnp.float32) - jnp.dot(
            block[...], x, preferred_element_type=jnp.float32
        )
        update(0, c, x)
        update(1, c, jnp.dot(
            other[...].reshape(snr, snr),
            segment.astype(jnp.bfloat16),
            preferred_element_type=jnp.float32,
        ).astype(jnp.bfloat16))
        candidate(2, c)

    def step(k, carry):
        for c in range(chunks):
            exchange(k, c)
            update(k, c, pick(k, c))

            @pl.when(k + 1 < sn)
            def _():
                candidate(k + 1, c)
        return carry

    lax.fori_loop(2, sn, step, 0)

    kept = solved.shape[0]
    begin = pl.multiple_of(z * kept, kept)
    for c in range(chunks):
        updated[:, c * BLK : (c + 1) * BLK] = running[c].astype(updated.dtype)
        solved[:, c * BLK : (c + 1) * BLK] = xs[c, pl.ds(begin, kept)]

    for d in range(1, n_src):
        inverse_copy(d, 0).wait_send()
        inverse_copy(d, 1).wait_send()
    for d in range(1, n_blk):
        block_copy(d).wait_send()
    for p in range(PIECES):
        message(FAR, sn, 0, p).wait_send()

        @pl.when(inner)
        def _():
            message(NEAR, sn, 0, p).wait_send()

    def drain(k, carry):
        for c in range(chunks):
            for p in range(PIECES):
                message(FAR, k, c, p).wait_send()

                @pl.when(inner)
                def _():
                    message(NEAR, k, c, p).wait_send()
        return carry

    lax.fori_loop(0, sn, drain, 0)


def pair_kernel(
    n_row, n_src,
    pattern_in, owners_in, offsets_in, rhs_in, factor, inverses_in, solved, updated,
    pattern, owners, offsets, rhs, panel, invs, running, xs,
    own, near, far_own, far_near, down_units, picked, blocks, lower,
    load_sem, panel_sem, inv_load, inv_send, inv_recv, blk_send, blk_recv,
    own_send, near_recv, far_own_recv, relay_send, far_near_recv, down_send, down_recv,
):
    chunks, rows, _ = running.shape
    snr = own.shape[1]
    sn = owners.shape[0]
    n_blk = snr // BLK
    part = snr // PIECES
    fac = chunks
    z = lax.axis_index("row")
    s = lax.axis_index("src")
    low = z < n_row // 2
    toward = jnp.where(low, 1, -1)
    far_dev = z + toward
    near_dev = z - toward
    at_end = (z == 0) | (z == n_row - 1)
    inner = jnp.logical_not(at_end)

    small = [
        pltpu.make_async_copy(source, target, load_sem.at[i])
        for i, (source, target) in enumerate((
            (owners_in, owners), (offsets_in, offsets), (rhs_in, rhs), (pattern_in, pattern),
        ))
    ]
    for load in small:
        load.start()
    inv_loads = [
        pltpu.make_async_copy(inverses_in.at[k], invs.at[k, s], inv_load.at[k]) for k in range(sn)
    ]
    loads = [
        pltpu.make_async_copy(factor.at[:, pl.ds(k * snr, snr)], panel.at[:, pl.ds(k * snr, snr)], panel_sem.at[k])
        for k in range(sn)
    ]
    for k in (0, 1):
        inv_loads[k].start()
    for k in (0, 2, 1, 3):
        loads[k].start()
    for k in (2, 3):
        inv_loads[k].start()

    barrier = pltpu.get_barrier_semaphore()
    pl.semaphore_signal(barrier, inc=1, device_id={"row": far_dev}, device_id_type=MESH)

    @pl.when(inner)
    def _():
        pl.semaphore_signal(barrier, inc=1, device_id={"row": near_dev}, device_id_type=MESH)

    for d in range(1, n_src):
        pl.semaphore_signal(
            barrier, inc=1, device_id={"src": lax.rem(s + d, n_src)}, device_id_type=MESH
        )

    for load in small[:3]:
        load.wait()
    mine = jnp.int32(sn)
    shift = jnp.int32(0)
    for k in range(sn):
        held = owners[k] == z
        mine = jnp.where(held, k, mine)
        shift = jnp.where(held, offsets[k], shift)

    def segment_of(read):
        found = read(0)
        for t in range(1, (rows - snr) // BLK + 1):
            found = jnp.where(shift == t, read(t * BLK), found)
        return found

    def raw(c):
        own[c] = segment_of(lambda t: rhs[t : t + snr, c * BLK : (c + 1) * BLK])

    def span(p):
        return pl.ds(p * part, part)

    def own_up(u, p):
        return pltpu.make_async_remote_copy(
            src_ref=own.at[u, span(p)], dst_ref=near.at[u, span(p)],
            send_sem=own_send.at[u, p], recv_sem=near_recv.at[u, p],
            device_id={"row": far_dev}, device_id_type=MESH,
        )

    def own_across(u, p):
        return pltpu.make_async_remote_copy(
            src_ref=own.at[u, span(p)], dst_ref=far_own.at[u, span(p)],
            send_sem=own_send.at[u, p], recv_sem=far_own_recv.at[u, p],
            device_id={"row": far_dev}, device_id_type=MESH,
        )

    def near_across(u, p):
        return pltpu.make_async_remote_copy(
            src_ref=near.at[u, span(p)], dst_ref=far_near.at[u, span(p)],
            send_sem=relay_send.at[u, p], recv_sem=far_near_recv.at[u, p],
            device_id={"row": far_dev}, device_id_type=MESH,
        )

    def from_near(u, p):
        return pltpu.make_async_remote_copy(
            src_ref=own.at[u, span(p)], dst_ref=near.at[u, span(p)],
            send_sem=own_send.at[u, p], recv_sem=near_recv.at[u, p],
            device_id={"row": near_dev}, device_id_type=MESH,
        )

    def down(u, q, p, to):
        return pltpu.make_async_remote_copy(
            src_ref=down_units.at[u, q, span(p)], dst_ref=down_units.at[u, q, span(p)],
            send_sem=down_send.at[u, q, p], recv_sem=down_recv.at[u, q, p],
            device_id={"row": to}, device_id_type=MESH,
        )

    def post_inner(u):
        @pl.when(inner)
        def _():
            for p in range(PIECES):
                own_across(u, p).start()

    def post_end(u):
        @pl.when(at_end)
        def _():
            for p in range(PIECES):
                own_up(u, p).start()

    def relay(u):
        @pl.when(inner)
        def _():
            for p in range(PIECES):
                from_near(u, p).wait_recv()
                near_across(u, p).start()

    def nodes(u):
        return (0, 1) if u < chunks else (1, 3) if u == fac else (2, 3)

    def holds(device, u):
        first, second = nodes(u)
        return (owners[first] == device) | (owners[second] == device)

    def down_early(u):
        @pl.when(inner)
        def _():
            use = holds(z, u)
            for p in range(PIECES):
                own_across(u, p).wait_recv()
                down_units[u, 0, span(p)] = jnp.where(use, own[u, span(p)], far_own[u, span(p)])
                down(u, 0, p, near_dev).start()

        @pl.when(at_end)
        def _():
            for p in range(PIECES):
                down(u, 0, p, far_dev).wait_recv()

    def down_late(u):
        @pl.when(inner)
        def _():
            use = holds(z + 2 * toward, u)
            for p in range(PIECES):
                near_across(u, p).wait_recv()
                down_units[u, 1, span(p)] = jnp.where(use, far_near[u, span(p)], far_own[u, span(p)])
                down(u, 1, p, near_dev).start()

        @pl.when(at_end)
        def _():
            for p in range(PIECES):
                down(u, 1, p, far_dev).wait_recv()

    def pick(u):
        @pl.when(inner)
        def _():
            for q, k in enumerate(nodes(u)):
                picked[q] = jnp.where(
                    mine == k,
                    own[u],
                    jnp.where(
                        owners[k] == near_dev,
                        near[u],
                        jnp.where(owners[k] == far_dev, far_own[u], far_near[u]),
                    ),
                )

        @pl.when(at_end)
        def _():
            for q, k in enumerate(nodes(u)):
                first = (owners[k] == far_dev) | (
                    (owners[k] == z + 2 * toward) & jnp.logical_not(holds(far_dev, u))
                )
                picked[q] = jnp.where(
                    mine == k, own[u], jnp.where(first, down_units[u, 0], down_units[u, 1])
                )

    def inverse_copy(d, k):
        return pltpu.make_async_remote_copy(
            src_ref=invs.at[k, s], dst_ref=invs.at[k, s],
            send_sem=inv_send.at[k, d], recv_sem=inv_recv.at[k, s],
            device_id={"src": lax.rem(s + d, n_src)}, device_id_type=MESH,
        )

    def inverse_arrival(d, k):
        source = lax.rem(s + n_src - d, n_src)
        return pltpu.make_async_remote_copy(
            src_ref=invs.at[k, source], dst_ref=invs.at[k, source],
            send_sem=inv_send.at[k, d], recv_sem=inv_recv.at[k, source],
            device_id={"src": source}, device_id_type=MESH,
        )

    def block_copy(d, q):
        return pltpu.make_async_remote_copy(
            src_ref=blocks.at[q, s], dst_ref=blocks.at[q, s],
            send_sem=blk_send.at[q, d], recv_sem=blk_recv.at[q, s],
            device_id={"src": lax.rem(s + d, n_src)}, device_id_type=MESH,
        )

    def block_arrival(d, q):
        source = lax.rem(s + n_src - d, n_src)
        return pltpu.make_async_remote_copy(
            src_ref=blocks.at[q, source], dst_ref=blocks.at[q, source],
            send_sem=blk_send.at[q, d], recv_sem=blk_recv.at[q, source],
            device_id={"src": source}, device_id_type=MESH,
        )

    def mask(k):
        loads[k].wait()
        for t in range(rows // BLK):
            inside = (t >= shift) & (t < shift + n_blk)
            rank = jnp.where(inside, mine, sn)
            for j in range(n_blk):
                keep = (pattern[t, k * n_blk + j] > 0) & (rank > k)
                at = (slice(t * BLK, (t + 1) * BLK), slice((k * n_blk + j) * BLK, (k * n_blk + j + 1) * BLK))
                tile = panel[at]
                panel[at] = jnp.where(keep, tile, jnp.zeros_like(tile))

    def inverse(k, value):
        return jnp.dot(
            invs[k].reshape(snr, snr), value, preferred_element_type=jnp.float32
        ).astype(jnp.bfloat16)

    def gathered(q):
        for d in range(1, n_src):
            block_arrival(d, q).wait_recv()
        for j in range(n_src):
            lower[q, :, j * BLK : (j + 1) * BLK] = blocks[q, j]
        for k in (2 * q, 2 * q + 1):
            for d in range(1, n_src):
                inverse_arrival(d, k).wait_recv()

    def solve(q, u, c):
        pick(u)
        first = inverse(2 * q, picked[0])
        segment = picked[1].astype(jnp.float32) - jnp.dot(
            lower[q], first, preferred_element_type=jnp.float32
        )
        second = inverse(2 * q + 1, segment.astype(jnp.bfloat16))
        begin = 2 * q * snr
        xs[c, begin : begin + snr] = first
        xs[c, begin + snr : begin + 2 * snr] = second
        running[c] = running[c] - jnp.dot(
            panel[:, begin : begin + 2 * snr], xs[c, begin : begin + 2 * snr],
            preferred_element_type=jnp.float32,
        )

    def early(c):
        solve(0, c, c)
        own[fac + 1 + c] = segment_of(lambda t: running[c, t : t + snr]).astype(jnp.bfloat16)
        post_inner(fac + 1 + c)
        post_end(fac + 1 + c)

    kept = solved.shape[0]

    def late(c):
        solve(1, fac + 1 + c, c)
        at = slice(c * BLK, (c + 1) * BLK)
        updated[:, at] = running[c].astype(updated.dtype)
        solved[:, at] = xs[c, pl.ds(pl.multiple_of(z * kept, kept), kept)]

    raw(0)
    pl.semaphore_wait(barrier, jnp.where(at_end, n_src, n_src + 1))
    post_inner(0)
    for k in (0, 1):
        inv_loads[k].wait()
        for d in range(1, n_src):
            inverse_copy(d, k).start()
    small[3].wait()
    mask(0)
    mask(2)
    columns = [pl.ds(pl.multiple_of((k * n_blk + s) * BLK, BLK), BLK) for k in (0, 2)]
    own[fac] = jnp.where(
        mine == 1,
        segment_of(lambda t: panel[t : t + snr, columns[0]]),
        segment_of(lambda t: panel[t : t + snr, columns[1]]),
    )
    post_inner(fac)
    post_end(fac)
    for c in range(1, chunks):
        raw(c)
    for c in range(chunks):
        post_end(c)
    mask(1)
    mask(3)
    for c in range(chunks):
        running[c] = rhs[:, c * BLK : (c + 1) * BLK].astype(jnp.float32)

    relay(fac)
    relay(0)
    down_early(0)
    down_early(fac)
    if chunks > 1:
        post_inner(1)
    down_late(fac)
    pick(fac)
    for q in range(2):
        blocks[q, s] = picked[q]
        for d in range(1, n_src):
            block_copy(d, q).start()
    for k in (2, 3):
        inv_loads[k].wait()
        for d in range(1, n_src):
            inverse_copy(d, k).start()
    for c in range(1, chunks):
        relay(c)
        if c + 1 < chunks:
            post_inner(c + 1)
        down_late(c - 1)
        if c + 1 < chunks:
            down_early(c)
    gathered(0)
    for c in range(chunks):
        if c == chunks - 1:
            if c > 0:
                down_early(c)
                early(c - 1)
            down_late(c)
            early(c)
        elif c < chunks - 2:
            early(c)
    for c in range(chunks):
        relay(fac + 1 + c)
        down_early(fac + 1 + c)
    gathered(1)
    for c in range(chunks):
        down_late(fac + 1 + c)
        late(c)

    for u in range(2 * chunks + 1):
        for p in range(PIECES):
            own_up(u, p).wait_send()

            @pl.when(inner)
            def _():
                near_across(u, p).wait_send()
                for q in range(2):
                    down(u, q, p, near_dev).wait_send()
    for d in range(1, n_src):
        for k in range(sn):
            inverse_copy(d, k).wait_send()
        for q in range(2):
            block_copy(d, q).wait_send()

def solution(mesh):
    n_row, n_src = mesh.shape["row"], mesh.shape["src"]

    def on_device(right_side, factor, pattern, inverses, owners, offsets):
        rows, cols = right_side.shape
        sn, inv_rows, snr = inverses.shape
        chunks = cols // BLK
        vmem = pl.BlockSpec(memory_space=pltpu.VMEM)
        hbm = pl.BlockSpec(memory_space=pltpu.HBM)
        kept = sn * snr // n_row
        if n_row == sn == 4 and n_src == snr // BLK:
            units = 2 * chunks + 1
            unit = (snr, BLK)
            pieces = pltpu.SemaphoreType.DMA((units, PIECES))
            return pl.pallas_call(
                functools.partial(pair_kernel, n_row, n_src),
                out_shape=(
                    jax.ShapeDtypeStruct((kept, cols), jnp.bfloat16),
                    jax.ShapeDtypeStruct((rows, cols), jnp.bfloat16),
                ),
                in_specs=[hbm] * 6,
                out_specs=(vmem, vmem),
                scratch_shapes=[
                    pltpu.SMEM(pattern.shape, jnp.int32),
                    pltpu.SMEM(owners.shape, jnp.int32),
                    pltpu.SMEM(offsets.shape, jnp.int32),
                    pltpu.VMEM(right_side.shape, jnp.bfloat16),
                    pltpu.VMEM(factor.shape, jnp.bfloat16),
                    pltpu.VMEM((sn, n_src, inv_rows, snr), jnp.bfloat16),
                    pltpu.VMEM((chunks, rows, BLK), jnp.float32),
                    pltpu.VMEM((chunks, sn * snr, BLK), jnp.bfloat16),
                    pltpu.VMEM((units, *unit), jnp.bfloat16),
                    pltpu.VMEM((units, *unit), jnp.bfloat16),
                    pltpu.VMEM((units, *unit), jnp.bfloat16),
                    pltpu.VMEM((units, *unit), jnp.bfloat16),
                    pltpu.VMEM((units, 2, *unit), jnp.bfloat16),
                    pltpu.VMEM((2, *unit), jnp.bfloat16),
                    pltpu.VMEM((2, n_src, *unit), jnp.bfloat16),
                    pltpu.VMEM((2, snr, snr), jnp.bfloat16),
                    pltpu.SemaphoreType.DMA((4,)),
                    pltpu.SemaphoreType.DMA((sn,)),
                    pltpu.SemaphoreType.DMA((sn,)),
                    pltpu.SemaphoreType.DMA((sn, n_src)),
                    pltpu.SemaphoreType.DMA((sn, n_src)),
                    pltpu.SemaphoreType.DMA((2, n_src)),
                    pltpu.SemaphoreType.DMA((2, n_src)),
                    pieces, pieces, pieces, pieces, pieces,
                    pltpu.SemaphoreType.DMA((units, 2, PIECES)),
                    pltpu.SemaphoreType.DMA((units, 2, PIECES)),
                ],
                compiler_params=pltpu.CompilerParams(
                    collective_id=0, has_side_effects=True, vmem_limit_bytes=63 * 1024 * 1024
                ),
            )(pattern, owners, offsets, right_side, factor, inverses)
        return pl.pallas_call(
            functools.partial(chain_kernel, n_row, n_src),
            out_shape=(
                jax.ShapeDtypeStruct((kept, cols), jnp.bfloat16),
                jax.ShapeDtypeStruct((rows, cols), jnp.bfloat16),
            ),
            in_specs=[hbm] * 6,
            out_specs=(vmem, vmem),
            scratch_shapes=[
                pltpu.SMEM(pattern.shape, jnp.int32),
                pltpu.SMEM(owners.shape, jnp.int32),
                pltpu.SMEM(offsets.shape, jnp.int32),
                pltpu.VMEM(right_side.shape, jnp.bfloat16),
                pltpu.VMEM(inverses.shape, jnp.bfloat16),
                pltpu.VMEM((sn, rows, snr), jnp.bfloat16),
                pltpu.VMEM((n_src, inv_rows, snr), jnp.bfloat16),
                pltpu.VMEM((chunks, rows, BLK), jnp.float32),
                pltpu.VMEM((sn + 1, chunks, snr, BLK), jnp.bfloat16),
                pltpu.VMEM((2, sn + 1, chunks, snr, BLK), jnp.bfloat16),
                pltpu.VMEM((2, sn + 1, chunks, snr, BLK), jnp.bfloat16),
                pltpu.VMEM((chunks, sn * snr, BLK), jnp.bfloat16),
                pltpu.VMEM((n_src, inv_rows, snr), jnp.bfloat16),
                pltpu.VMEM((chunks, snr, BLK), jnp.bfloat16),
                pltpu.VMEM((snr // BLK, snr, BLK), jnp.bfloat16),
                pltpu.VMEM((snr, snr), jnp.bfloat16),
                pltpu.SemaphoreType.DMA((5,)),
                pltpu.SemaphoreType.DMA((sn,)),
                pltpu.SemaphoreType.DMA((2, n_src)),
                pltpu.SemaphoreType.DMA((2, n_src)),
                pltpu.SemaphoreType.DMA((snr // BLK,)),
                pltpu.SemaphoreType.DMA((snr // BLK,)),
                pltpu.SemaphoreType.DMA((2, sn + 1, chunks, PIECES)),
                pltpu.SemaphoreType.DMA((2, sn + 1, chunks, PIECES)),
            ],
            compiler_params=pltpu.CompilerParams(
                collective_id=0, has_side_effects=True, vmem_limit_bytes=63 * 1024 * 1024
            ),
        )(pattern, owners, offsets, right_side, factor, inverses)

    return jax.shard_map(
        on_device,
        mesh=mesh,
        in_specs=(
            P(("group", "row"), "src"),
            P(("group", "row"), None),
            P(("group", "row"), None),
            P("group", "src", None),
            P("group"),
            P("group"),
        ),
        out_specs=(P(("group", "row"), "src"), P(("group", "row"), "src")),
        check_vma=False,
    )
```

```python
import functools

import jax
import jax.numpy as jnp
from jax import lax
from jax.experimental import pallas as pl
from jax.experimental.pallas import tpu as pltpu
from jax.sharding import PartitionSpec as P

BLK = 128
PIECES = 2
AHEAD = 4
NEAR, FAR = 0, 1
MESH = pl.DeviceIdType.MESH


def chain_kernel(
    n_row, n_src,
    pattern_in, owners_in, offsets_in, rhs_in, factor, inverses_in, solved, updated,
    pattern, owners, offsets, rhs, inverses,
    panel, whole, running, cand, recv, out, xs,
    other, first, blocks, block,
    load_sem, panel_sem, inv_send, inv_recv, blk_send, blk_recv, send_sem, recv_sem,
):
    sn, rows, snr = panel.shape
    chunks = running.shape[0]
    part = snr // PIECES
    z = lax.axis_index("row")
    s = lax.axis_index("src")
    low = z < n_row // 2
    toward = jnp.where(low, 1, -1)
    far_dev = z + toward
    near_dev = z - toward
    at_end = (z == 0) | (z == n_row - 1)
    inner = jnp.logical_not(at_end)
    crossing = (z == n_row // 2 - 1) | (z == n_row // 2)
    far_slot = jnp.where(crossing, FAR, NEAR)

    small = [
        pltpu.make_async_copy(source, target, load_sem.at[i])
        for i, (source, target) in enumerate((
            (owners_in, owners), (offsets_in, offsets), (pattern_in, pattern),
            (inverses_in, inverses), (rhs_in, rhs),
        ))
    ]
    for load in small:
        load.start()
    loads = [
        pltpu.make_async_copy(factor.at[:, pl.ds(k * snr, snr)], panel.at[k], panel_sem.at[k])
        for k in range(sn)
    ]
    for load in loads:
        load.start()

    barrier = pltpu.get_barrier_semaphore()
    pl.semaphore_signal(barrier, inc=1, device_id={"row": far_dev}, device_id_type=MESH)

    @pl.when(inner)
    def _():
        pl.semaphore_signal(barrier, inc=1, device_id={"row": near_dev}, device_id_type=MESH)

    for d in range(1, n_src):
        pl.semaphore_signal(
            barrier, inc=1, device_id={"src": lax.rem(s + d, n_src)}, device_id_type=MESH
        )

    for load in small:
        load.wait()
    mine = jnp.int32(sn)
    shift = jnp.int32(0)
    for k in range(sn):
        held = owners[k] == z
        mine = jnp.where(held, k, mine)
        shift = jnp.where(held, offsets[k], shift)
    own_rows = inverses[0]
    for k in range(1, sn):
        own_rows = jnp.where(mine == k, inverses[k], own_rows)
    whole[s] = own_rows
    for c in range(chunks):
        running[c] = rhs[:, c * BLK : (c + 1) * BLK].astype(jnp.float32)

    pl.semaphore_wait(barrier, jnp.where(at_end, n_src, n_src + 1))

    def inverse_copy(d, which):
        return pltpu.make_async_remote_copy(
            src_ref=inverses.at[1] if which else whole.at[s],
            dst_ref=other.at[s] if which else whole.at[s],
            send_sem=inv_send.at[which, d],
            recv_sem=inv_recv.at[which, s],
            device_id={"src": lax.rem(s + d, n_src)},
            device_id_type=MESH,
        )

    def inverse_arrival(d, which):
        source = lax.rem(s + n_src - d, n_src)
        held = other if which else whole
        return pltpu.make_async_remote_copy(
            src_ref=held.at[source],
            dst_ref=held.at[source],
            send_sem=inv_send.at[which, d],
            recv_sem=inv_recv.at[which, source],
            device_id={"src": source},
            device_id_type=MESH,
        )

    n_blk = snr // BLK
    b = lax.rem(s, n_blk)

    def block_copy(d):
        return pltpu.make_async_remote_copy(
            src_ref=blocks.at[b],
            dst_ref=blocks.at[b],
            send_sem=blk_send.at[d],
            recv_sem=blk_recv.at[b],
            device_id={"src": s - b + lax.rem(b + d, n_blk)},
            device_id_type=MESH,
        )

    def block_arrival(d):
        source = lax.rem(b + n_blk - d, n_blk)
        return pltpu.make_async_remote_copy(
            src_ref=blocks.at[source],
            dst_ref=blocks.at[source],
            send_sem=blk_send.at[d],
            recv_sem=blk_recv.at[source],
            device_id={"src": s - b + source},
            device_id_type=MESH,
        )

    for d in range(1, n_src):
        inverse_copy(d, 0).start()
    for d in range(1, n_src):
        inverse_copy(d, 1).start()
    other[s] = inverses[1]

    def mask(k):
        loads[k].wait()
        for t in range(rows // BLK):
            inside = (t >= shift) & (t < shift + snr // BLK)
            rank = jnp.where(inside, mine, sn)
            for j in range(snr // BLK):
                keep = (pattern[t, k * (snr // BLK) + j] > 0) & (rank > k)
                tile = panel[k, t * BLK : (t + 1) * BLK, j * BLK : (j + 1) * BLK]
                panel[k, t * BLK : (t + 1) * BLK, j * BLK : (j + 1) * BLK] = jnp.where(
                    keep, tile, jnp.zeros_like(tile)
                )

    def message(way, k, c, p):
        span = pl.ds(p * part, part)
        return pltpu.make_async_remote_copy(
            src_ref=out.at[way, k, c, span],
            dst_ref=recv.at[far_slot if way == FAR else FAR, k, c, span],
            send_sem=send_sem.at[way, k, c, p],
            recv_sem=recv_sem.at[far_slot if way == FAR else FAR, k, c, p],
            device_id={"row": far_dev if way == FAR else near_dev},
            device_id_type=MESH,
        )

    def arrival(way, k, c, p):
        span = pl.ds(p * part, part)
        return pltpu.make_async_remote_copy(
            src_ref=out.at[way, k, c, span],
            dst_ref=recv.at[way, k, c, span],
            send_sem=send_sem.at[way, k, c, p],
            recv_sem=recv_sem.at[way, k, c, p],
            device_id={"row": far_dev if way == FAR else near_dev},
            device_id_type=MESH,
        )

    def offer(k, c, value):
        cand[k, c] = value

        @pl.when(at_end)
        def _():
            out[FAR, k, c] = value
            for p in range(PIECES):
                message(FAR, k, c, p).start()

    def segment_of(read):
        found = read(0)
        for t in range(1, (rows - snr) // BLK + 1):
            found = jnp.where(shift == t, read(t * BLK), found)
        return found

    def own_segment(c):
        return segment_of(lambda t: running[c, t : t + snr]).astype(jnp.bfloat16)

    def candidate(k, c):
        offer(k, c, jnp.dot(
            whole[...].reshape(snr, snr), own_segment(c), preferred_element_type=jnp.float32
        ).astype(jnp.bfloat16))

    def node(k):
        if isinstance(k, int):
            return (1, 0)[k] if k < 2 else 1 if k == sn else k
        return k

    def forward(k, c, p, came, way):
        arrival(came, k, c, p).wait_recv()
        span = pl.ds(p * part, part)
        out[way, k, c, span] = jnp.where(
            mine == node(k), cand[k, c, span], recv[came, k, c, span]
        )
        message(way, k, c, p).start()

    opening = [(sn, 0)] + [(k, c) for c in range(chunks) for k in (0, 1)]

    def near_forward(k, place):
        c, p = divmod(place, PIECES)
        if isinstance(k, int):
            later = opening.index((k, 0)) + c if k == sn else c
            k, c = opening[later] if later < len(opening) else (2, later - len(opening))
            forward(k, c, p, NEAR, FAR)
        elif c < chunks:
            forward(k, c, p, NEAR, FAR)
        else:
            @pl.when(k + 1 < sn)
            def _():
                forward(k + 1, c - chunks, p, NEAR, FAR)

    def exchange(k, c):
        @pl.when(inner)
        def _():
            for p in range(PIECES):
                base = opening.index((k, c)) if isinstance(k, int) else c
                near_forward(sn if isinstance(k, int) else k, base * PIECES + p + AHEAD)
                forward(k, c, p, FAR, NEAR)

        @pl.when(at_end)
        def _():
            for p in range(PIECES):
                arrival(FAR, k, c, p).wait_recv()

    def pick(k, c):
        owner = owners[node(k)]
        from_near = jnp.where(low, z - owner, owner - z) > 0
        return jnp.where(
            mine == node(k),
            cand[k, c],
            jnp.where(from_near, recv[NEAR, k, c], recv[FAR, k, c]),
        )

    def update(k, c, x):
        begin = k * snr if isinstance(k, int) else pl.multiple_of(k * snr, snr)
        xs[c, pl.ds(begin, snr)] = x
        running[c] = running[c] - jnp.dot(panel[k], x, preferred_element_type=jnp.float32)

    @pl.when(at_end)
    def _():
        recv[NEAR] = jnp.zeros_like(recv[NEAR])

    mask(0)
    stored = segment_of(lambda t: panel[0, t : t + snr, :BLK])
    for j in range(1, n_blk):
        column = segment_of(lambda t: panel[0, t : t + snr, j * BLK : (j + 1) * BLK])
        stored = jnp.where(b == j, column, stored)
    offer(sn, 0, stored)
    offer(0, 0, own_segment(0))
    for d in range(1, n_src):
        inverse_arrival(d, 0).wait_recv()
    for c in range(chunks):
        if c > 0:
            offer(0, c, own_segment(c))
        candidate(1, c)

    @pl.when(inner)
    def _():
        for place in range(AHEAD):
            near_forward(sn, place)

    exchange(sn, 0)
    blocks[b] = pick(sn, 0)
    for d in range(1, n_blk):
        block_copy(d).start()
    for k in range(1, sn):
        mask(k)
    for c in range(chunks):
        exchange(0, c)
        first[c] = pick(0, c)
        exchange(1, c)
        if c == 0:
            for d in range(1, n_src):
                inverse_arrival(d, 1).wait_recv()
            for d in range(1, n_blk):
                block_arrival(d).wait_recv()
            for j in range(n_blk):
                block[:, j * BLK : (j + 1) * BLK] = blocks[j]
        x = pick(1, c)
        segment = first[c].astype(jnp.float32) - jnp.dot(
            block[...], x, preferred_element_type=jnp.float32
        )
        update(0, c, x)
        update(1, c, jnp.dot(
            other[...].reshape(snr, snr),
            segment.astype(jnp.bfloat16),
            preferred_element_type=jnp.float32,
        ).astype(jnp.bfloat16))
        candidate(2, c)

    def step(k, carry):
        for c in range(chunks):
            exchange(k, c)
            update(k, c, pick(k, c))

            @pl.when(k + 1 < sn)
            def _():
                candidate(k + 1, c)
        return carry

    lax.fori_loop(2, sn, step, 0)

    kept = solved.shape[0]
    begin = pl.multiple_of(z * kept, kept)
    for c in range(chunks):
        updated[:, c * BLK : (c + 1) * BLK] = running[c].astype(updated.dtype)
        solved[:, c * BLK : (c + 1) * BLK] = xs[c, pl.ds(begin, kept)]

    for d in range(1, n_src):
        inverse_copy(d, 0).wait_send()
        inverse_copy(d, 1).wait_send()
    for d in range(1, n_blk):
        block_copy(d).wait_send()
    for p in range(PIECES):
        message(FAR, sn, 0, p).wait_send()

        @pl.when(inner)
        def _():
            message(NEAR, sn, 0, p).wait_send()

    def drain(k, carry):
        for c in range(chunks):
            for p in range(PIECES):
                message(FAR, k, c, p).wait_send()

                @pl.when(inner)
                def _():
                    message(NEAR, k, c, p).wait_send()
        return carry

    lax.fori_loop(0, sn, drain, 0)


def pair_kernel(
    n_row, n_src,
    pattern, owners, offsets, rhs_in, factor, inverses_in, solved, updated,
    rhs, panel, invs, running, xs,
    own, near, far_own, far_near, down_units, picked, blocks, lower,
    load_sem, panel_sem, inv_load, inv_send, inv_recv, blk_send, blk_recv,
    own_send, near_recv, far_own_recv, relay_send, far_near_recv, down_send, down_recv,
):
    chunks, rows, _ = running.shape
    snr = own.shape[1]
    sn = owners.shape[0]
    n_blk = snr // BLK
    part = snr // PIECES
    fac = chunks
    z = lax.axis_index("row")
    s = lax.axis_index("src")
    low = z < n_row // 2
    toward = jnp.where(low, 1, -1)
    far_dev = z + toward
    near_dev = z - toward
    at_end = (z == 0) | (z == n_row - 1)
    inner = jnp.logical_not(at_end)

    small = [
        pltpu.make_async_copy(source, target, load_sem.at[i])
        for i, (source, target) in enumerate(((rhs_in, rhs),))
    ]
    for load in small:
        load.start()
    inv_loads = [
        pltpu.make_async_copy(inverses_in.at[k], invs.at[k, s], inv_load.at[k]) for k in range(sn)
    ]
    loads = [
        pltpu.make_async_copy(factor.at[:, pl.ds(k * snr, snr)], panel.at[:, pl.ds(k * snr, snr)], panel_sem.at[k])
        for k in range(sn)
    ]
    for k in (0, 1):
        inv_loads[k].start()
    for k in (0, 2, 1, 3):
        loads[k].start()
    for k in (2, 3):
        inv_loads[k].start()

    barrier = pltpu.get_barrier_semaphore()
    pl.semaphore_signal(barrier, inc=1, device_id={"row": far_dev}, device_id_type=MESH)

    @pl.when(inner)
    def _():
        pl.semaphore_signal(barrier, inc=1, device_id={"row": near_dev}, device_id_type=MESH)

    for d in range(1, n_src):
        pl.semaphore_signal(
            barrier, inc=1, device_id={"src": lax.rem(s + d, n_src)}, device_id_type=MESH
        )

    for load in small:
        load.wait()
    mine = jnp.int32(sn)
    shift = jnp.int32(0)
    for k in range(sn):
        held = owners[k] == z
        mine = jnp.where(held, k, mine)
        shift = jnp.where(held, offsets[k], shift)

    def segment_of(read):
        found = read(0)
        for t in range(1, (rows - snr) // BLK + 1):
            found = jnp.where(shift == t, read(t * BLK), found)
        return found

    def raw(c):
        own[c] = segment_of(lambda t: rhs[t : t + snr, c * BLK : (c + 1) * BLK])

    def span(p):
        return pl.ds(p * part, part)

    def own_up(u, p):
        return pltpu.make_async_remote_copy(
            src_ref=own.at[u, span(p)], dst_ref=near.at[u, span(p)],
            send_sem=own_send.at[u, p], recv_sem=near_recv.at[u, p],
            device_id={"row": far_dev}, device_id_type=MESH,
        )

    def own_across(u, p):
        return pltpu.make_async_remote_copy(
            src_ref=own.at[u, span(p)], dst_ref=far_own.at[u, span(p)],
            send_sem=own_send.at[u, p], recv_sem=far_own_recv.at[u, p],
            device_id={"row": far_dev}, device_id_type=MESH,
        )

    def near_across(u, p):
        return pltpu.make_async_remote_copy(
            src_ref=near.at[u, span(p)], dst_ref=far_near.at[u, span(p)],
            send_sem=relay_send.at[u, p], recv_sem=far_near_recv.at[u, p],
            device_id={"row": far_dev}, device_id_type=MESH,
        )

    def from_near(u, p):
        return pltpu.make_async_remote_copy(
            src_ref=own.at[u, span(p)], dst_ref=near.at[u, span(p)],
            send_sem=own_send.at[u, p], recv_sem=near_recv.at[u, p],
            device_id={"row": near_dev}, device_id_type=MESH,
        )

    def down(u, q, p, to):
        return pltpu.make_async_remote_copy(
            src_ref=down_units.at[u, q, span(p)], dst_ref=down_units.at[u, q, span(p)],
            send_sem=down_send.at[u, q, p], recv_sem=down_recv.at[u, q, p],
            device_id={"row": to}, device_id_type=MESH,
        )

    def post_inner(u):
        @pl.when(inner)
        def _():
            for p in range(PIECES):
                own_across(u, p).start()

    def post_end(u):
        @pl.when(at_end)
        def _():
            for p in range(PIECES):
                own_up(u, p).start()

    def relay(u):
        @pl.when(inner)
        def _():
            for p in range(PIECES):
                from_near(u, p).wait_recv()
                near_across(u, p).start()

    def nodes(u):
        return (0, 1) if u < chunks else (1, 3) if u == fac else (2, 3)

    def holds(device, u):
        first, second = nodes(u)
        return (owners[first] == device) | (owners[second] == device)

    def down_early(u):
        @pl.when(inner)
        def _():
            use = holds(z, u)
            for p in range(PIECES):
                own_across(u, p).wait_recv()
                down_units[u, 0, span(p)] = jnp.where(use, own[u, span(p)], far_own[u, span(p)])
                down(u, 0, p, near_dev).start()

        @pl.when(at_end)
        def _():
            for p in range(PIECES):
                down(u, 0, p, far_dev).wait_recv()

    def down_late(u):
        @pl.when(inner)
        def _():
            use = holds(z + 2 * toward, u)
            for p in range(PIECES):
                near_across(u, p).wait_recv()
                down_units[u, 1, span(p)] = jnp.where(use, far_near[u, span(p)], far_own[u, span(p)])
                down(u, 1, p, near_dev).start()

        @pl.when(at_end)
        def _():
            for p in range(PIECES):
                down(u, 1, p, far_dev).wait_recv()

    def pick(u):
        @pl.when(inner)
        def _():
            for q, k in enumerate(nodes(u)):
                picked[q] = jnp.where(
                    mine == k,
                    own[u],
                    jnp.where(
                        owners[k] == near_dev,
                        near[u],
                        jnp.where(owners[k] == far_dev, far_own[u], far_near[u]),
                    ),
                )

        @pl.when(at_end)
        def _():
            for q, k in enumerate(nodes(u)):
                first = (owners[k] == far_dev) | (
                    (owners[k] == z + 2 * toward) & jnp.logical_not(holds(far_dev, u))
                )
                picked[q] = jnp.where(
                    mine == k, own[u], jnp.where(first, down_units[u, 0], down_units[u, 1])
                )

    def inverse_copy(d, k):
        return pltpu.make_async_remote_copy(
            src_ref=invs.at[k, s], dst_ref=invs.at[k, s],
            send_sem=inv_send.at[k, d], recv_sem=inv_recv.at[k, s],
            device_id={"src": lax.rem(s + d, n_src)}, device_id_type=MESH,
        )

    def inverse_arrival(d, k):
        source = lax.rem(s + n_src - d, n_src)
        return pltpu.make_async_remote_copy(
            src_ref=invs.at[k, source], dst_ref=invs.at[k, source],
            send_sem=inv_send.at[k, d], recv_sem=inv_recv.at[k, source],
            device_id={"src": source}, device_id_type=MESH,
        )

    def block_copy(d, q):
        return pltpu.make_async_remote_copy(
            src_ref=blocks.at[q, s], dst_ref=blocks.at[q, s],
            send_sem=blk_send.at[q, d], recv_sem=blk_recv.at[q, s],
            device_id={"src": lax.rem(s + d, n_src)}, device_id_type=MESH,
        )

    def block_arrival(d, q):
        source = lax.rem(s + n_src - d, n_src)
        return pltpu.make_async_remote_copy(
            src_ref=blocks.at[q, source], dst_ref=blocks.at[q, source],
            send_sem=blk_send.at[q, d], recv_sem=blk_recv.at[q, source],
            device_id={"src": source}, device_id_type=MESH,
        )

    def mask(k):
        loads[k].wait()
        for t in range(rows // BLK):
            inside = (t >= shift) & (t < shift + n_blk)
            rank = jnp.where(inside, mine, sn)
            for j in range(n_blk):
                keep = (pattern[t, k * n_blk + j] > 0) & (rank > k)
                at = (slice(t * BLK, (t + 1) * BLK), slice((k * n_blk + j) * BLK, (k * n_blk + j + 1) * BLK))
                tile = panel[at]
                panel[at] = jnp.where(keep, tile, jnp.zeros_like(tile))

    def inverse(k, value):
        return jnp.dot(
            invs[k].reshape(snr, snr), value, preferred_element_type=jnp.float32
        ).astype(jnp.bfloat16)

    def gathered(q):
        for d in range(1, n_src):
            block_arrival(d, q).wait_recv()
        for j in range(n_src):
            lower[q, :, j * BLK : (j + 1) * BLK] = blocks[q, j]
        for k in (2 * q, 2 * q + 1):
            for d in range(1, n_src):
                inverse_arrival(d, k).wait_recv()

    def solve(q, u, c):
        pick(u)
        first = inverse(2 * q, picked[0])
        segment = picked[1].astype(jnp.float32) - jnp.dot(
            lower[q], first, preferred_element_type=jnp.float32
        )
        second = inverse(2 * q + 1, segment.astype(jnp.bfloat16))
        begin = 2 * q * snr
        xs[c, begin : begin + snr] = first
        xs[c, begin + snr : begin + 2 * snr] = second
        running[c] = running[c] - jnp.dot(
            panel[:, begin : begin + 2 * snr], xs[c, begin : begin + 2 * snr],
            preferred_element_type=jnp.float32,
        )

    def early(c):
        solve(0, c, c)
        own[fac + 1 + c] = segment_of(lambda t: running[c, t : t + snr]).astype(jnp.bfloat16)
        post_inner(fac + 1 + c)
        post_end(fac + 1 + c)

    kept = solved.shape[0]

    def late(c):
        solve(1, fac + 1 + c, c)
        at = slice(c * BLK, (c + 1) * BLK)
        updated[:, at] = running[c].astype(updated.dtype)
        solved[:, at] = xs[c, pl.ds(pl.multiple_of(z * kept, kept), kept)]

    raw(0)
    pl.semaphore_wait(barrier, jnp.where(at_end, n_src, n_src + 1))
    post_inner(0)
    for k in (0, 1):
        inv_loads[k].wait()
        for d in range(1, n_src):
            inverse_copy(d, k).start()
    mask(0)
    mask(2)
    columns = [pl.ds(pl.multiple_of((k * n_blk + s) * BLK, BLK), BLK) for k in (0, 2)]
    own[fac] = jnp.where(
        mine == 1,
        segment_of(lambda t: panel[t : t + snr, columns[0]]),
        segment_of(lambda t: panel[t : t + snr, columns[1]]),
    )
    post_inner(fac)
    post_end(fac)
    for c in range(1, chunks):
        raw(c)
    for c in range(chunks):
        post_end(c)
    mask(1)
    mask(3)
    for c in range(chunks):
        running[c] = rhs[:, c * BLK : (c + 1) * BLK].astype(jnp.float32)

    relay(fac)
    down_early(0)
    relay(0)
    if chunks > 1:
        post_inner(1)
    down_early(fac)
    down_late(fac)
    pick(fac)
    for q in range(2):
        blocks[q, s] = picked[q]
        for d in range(1, n_src):
            block_copy(d, q).start()
    for k in (2, 3):
        inv_loads[k].wait()
        for d in range(1, n_src):
            inverse_copy(d, k).start()
    for c in range(1, chunks):
        relay(c)
        if c + 1 < chunks:
            post_inner(c + 1)
        down_late(c - 1)
        if c + 1 < chunks:
            down_early(c)
    gathered(0)
    for c in range(chunks):
        if c == chunks - 1:
            if c > 0:
                down_early(c)
                early(c - 1)
            down_late(c)
            early(c)
        elif c < chunks - 2:
            early(c)
    for c in range(chunks):
        down_early(fac + 1 + c)
        relay(fac + 1 + c)
    gathered(1)
    for c in range(chunks):
        down_late(fac + 1 + c)
        late(c)

    for u in range(2 * chunks + 1):
        for p in range(PIECES):
            own_up(u, p).wait_send()

            @pl.when(inner)
            def _():
                near_across(u, p).wait_send()
                for q in range(2):
                    down(u, q, p, near_dev).wait_send()
    for d in range(1, n_src):
        for k in range(sn):
            inverse_copy(d, k).wait_send()
        for q in range(2):
            block_copy(d, q).wait_send()

def solution(mesh):
    n_row, n_src = mesh.shape["row"], mesh.shape["src"]

    def on_device(right_side, factor, pattern, inverses, owners, offsets):
        rows, cols = right_side.shape
        sn, inv_rows, snr = inverses.shape
        chunks = cols // BLK
        vmem = pl.BlockSpec(memory_space=pltpu.VMEM)
        hbm = pl.BlockSpec(memory_space=pltpu.HBM)
        kept = sn * snr // n_row
        if n_row == sn == 4 and n_src == snr // BLK:
            units = 2 * chunks + 1
            unit = (snr, BLK)
            pieces = pltpu.SemaphoreType.DMA((units, PIECES))
            return pl.pallas_call(
                functools.partial(pair_kernel, n_row, n_src),
                out_shape=(
                    jax.ShapeDtypeStruct((kept, cols), jnp.bfloat16),
                    jax.ShapeDtypeStruct((rows, cols), jnp.bfloat16),
                ),
                in_specs=[pl.BlockSpec(memory_space=pltpu.SMEM)] * 3 + [hbm] * 3,
                out_specs=(vmem, vmem),
                scratch_shapes=[
                    pltpu.VMEM(right_side.shape, jnp.bfloat16),
                    pltpu.VMEM(factor.shape, jnp.bfloat16),
                    pltpu.VMEM((sn, n_src, inv_rows, snr), jnp.bfloat16),
                    pltpu.VMEM((chunks, rows, BLK), jnp.float32),
                    pltpu.VMEM((chunks, sn * snr, BLK), jnp.bfloat16),
                    pltpu.VMEM((units, *unit), jnp.bfloat16),
                    pltpu.VMEM((units, *unit), jnp.bfloat16),
                    pltpu.VMEM((units, *unit), jnp.bfloat16),
                    pltpu.VMEM((units, *unit), jnp.bfloat16),
                    pltpu.VMEM((units, 2, *unit), jnp.bfloat16),
                    pltpu.VMEM((2, *unit), jnp.bfloat16),
                    pltpu.VMEM((2, n_src, *unit), jnp.bfloat16),
                    pltpu.VMEM((2, snr, snr), jnp.bfloat16),
                    pltpu.SemaphoreType.DMA((1,)),
                    pltpu.SemaphoreType.DMA((sn,)),
                    pltpu.SemaphoreType.DMA((sn,)),
                    pltpu.SemaphoreType.DMA((sn, n_src)),
                    pltpu.SemaphoreType.DMA((sn, n_src)),
                    pltpu.SemaphoreType.DMA((2, n_src)),
                    pltpu.SemaphoreType.DMA((2, n_src)),
                    pieces, pieces, pieces, pieces, pieces,
                    pltpu.SemaphoreType.DMA((units, 2, PIECES)),
                    pltpu.SemaphoreType.DMA((units, 2, PIECES)),
                ],
                compiler_params=pltpu.CompilerParams(
                    collective_id=0, has_side_effects=True, vmem_limit_bytes=53 * 1024 * 1024
                ),
            )(pattern, owners, offsets, right_side, factor, inverses)
        return pl.pallas_call(
            functools.partial(chain_kernel, n_row, n_src),
            out_shape=(
                jax.ShapeDtypeStruct((kept, cols), jnp.bfloat16),
                jax.ShapeDtypeStruct((rows, cols), jnp.bfloat16),
            ),
            in_specs=[hbm] * 6,
            out_specs=(vmem, vmem),
            scratch_shapes=[
                pltpu.SMEM(pattern.shape, jnp.int32),
                pltpu.SMEM(owners.shape, jnp.int32),
                pltpu.SMEM(offsets.shape, jnp.int32),
                pltpu.VMEM(right_side.shape, jnp.bfloat16),
                pltpu.VMEM(inverses.shape, jnp.bfloat16),
                pltpu.VMEM((sn, rows, snr), jnp.bfloat16),
                pltpu.VMEM((n_src, inv_rows, snr), jnp.bfloat16),
                pltpu.VMEM((chunks, rows, BLK), jnp.float32),
                pltpu.VMEM((sn + 1, chunks, snr, BLK), jnp.bfloat16),
                pltpu.VMEM((2, sn + 1, chunks, snr, BLK), jnp.bfloat16),
                pltpu.VMEM((2, sn + 1, chunks, snr, BLK), jnp.bfloat16),
                pltpu.VMEM((chunks, sn * snr, BLK), jnp.bfloat16),
                pltpu.VMEM((n_src, inv_rows, snr), jnp.bfloat16),
                pltpu.VMEM((chunks, snr, BLK), jnp.bfloat16),
                pltpu.VMEM((snr // BLK, snr, BLK), jnp.bfloat16),
                pltpu.VMEM((snr, snr), jnp.bfloat16),
                pltpu.SemaphoreType.DMA((5,)),
                pltpu.SemaphoreType.DMA((sn,)),
                pltpu.SemaphoreType.DMA((2, n_src)),
                pltpu.SemaphoreType.DMA((2, n_src)),
                pltpu.SemaphoreType.DMA((snr // BLK,)),
                pltpu.SemaphoreType.DMA((snr // BLK,)),
                pltpu.SemaphoreType.DMA((2, sn + 1, chunks, PIECES)),
                pltpu.SemaphoreType.DMA((2, sn + 1, chunks, PIECES)),
            ],
            compiler_params=pltpu.CompilerParams(
                collective_id=0, has_side_effects=True, vmem_limit_bytes=63 * 1024 * 1024
            ),
        )(pattern, owners, offsets, right_side, factor, inverses)

    return jax.shard_map(
        on_device,
        mesh=mesh,
        in_specs=(
            P(("group", "row"), "src"),
            P(("group", "row"), None),
            P(("group", "row"), None),
            P("group", "src", None),
            P("group"),
            P("group"),
        ),
        out_specs=(P(("group", "row"), "src"), P(("group", "row"), "src")),
        check_vma=False,
    )
```
